32 devices in a mesh: pb: 8 (over y, x, core), kv: 4 (over z).
Axes of the slice: x: 2, y: 2, z: 4, core: 2. Of those that a mesh axis runs over, the one named last changes fastest.
Arguments:
- queries: bfloat16 [4096, 1024], P(('pb', 'kv')), may hold values from -6 to 6
- key_rows: bfloat16 [4096, 128], P(('kv', 'pb')), may hold values from -6 to 6
- value_rows: bfloat16 [4096, 128], P(('kv', 'pb')), may hold values from -0.59765625 to 0.59765625
- output: bfloat16 [4096, 1024], P(('pb', 'kv')), may hold values from -1.796875 to 1.796875
- out_grad: bfloat16 [4096, 1024], P(('pb', 'kv')), may hold values from -6 to 6
- log_norm: float32 [8, 4096], P(None, ('pb', 'kv')), as said below
- positions: int32 [4096], replicated, may hold values from 0 to 4095, as said below
Outputs:
- query_grad: float32 [4096, 1024], P(('pb', 'kv'))
- key_grad: float32 [4096, 128], P(('kv', 'pb'))
- value_grad: float32 [4096, 128], P(('kv', 'pb'))
The draws below stay inside these ranges and needn't reach their ends.
Inputs may be any that keep to these rules, and one draw needn't show every extreme that they name: A permutation of 0 to 4095: row r holds the token at position positions[r]. log_norm[h, r] - log(1 + positions[r]) lies between 0.25 and 0.75.
All inputs are finite; a program needn't handle non-finite values.
Results may differ from the reference program's by a relative error of at most 0.0041.
Values may be sent and summed in bfloat16 or wider, within the bound.
A program may use at most 64 MiB of HBM per device.

```python
import math
import jax
import jax.numpy as jnp
from jax import lax

HD = 128
GROUP = 8
S = 4096
QTOK = 512
N_PB = 8


def shared_order(key):
    return jax.random.permutation(jax.random.fold_in(key, 7), S).astype(jnp.int32)


def draw_positions(key, part):
    return shared_order(key)


def draw_log_norm(key, part):
    token_pos = shared_order(key).astype(jnp.float32)
    offset_key = jax.random.fold_in(key, 9)
    offsets = jax.random.uniform(offset_key, (GROUP, S), jnp.float32, 0.25, 0.75)
    return jnp.log(token_pos + 1.0)[None, :] + offsets


def level_of(rng, dims, pieces, low, largest):
    level, own = 1.0, jax.random.fold_in(rng, 6)
    for position, parts in pieces:
        steps = jnp.exp(jax.random.uniform(jax.random.fold_in(own, position), (parts,), jnp.float32, low / len(pieces), largest / len(pieces)))
        level = level * jnp.repeat(steps, dims[position] // parts).reshape([-1 if axis == position else 1 for axis in range(len(dims))])
    return level


def noise(key, dims, spread, bound, shards=(), held_as=jnp.bfloat16):
    entries = jax.random.normal(key, dims, jnp.float32) * spread
    if len(shards) > 0:
        entries = level_of(key, dims, shards, -0.22, 0.18) * entries
    return jnp.clip(entries, min=-bound, max=bound).astype(held_as)


def setup_inputs(seed: int = 0) -> dict:
    key_list = jax.random.split(jax.random.key(seed), 8)
    return {
        "queries": noise(key_list[0], (S, GROUP * HD), 1.0, 6.0, ((0, 32),)),
        "key_rows": noise(key_list[1], (S, HD), 1.0, 6.0, ((0, 32),)),
        "value_rows": noise(key_list[2], (S, HD), 0.1, 0.59765625, ((0, 32),)),
        "output": noise(key_list[3], (S, GROUP * HD), 0.3, 1.796875, ((0, 32),)),
        "out_grad": noise(key_list[4], (S, GROUP * HD), 1.0, 6.0, ((0, 32),)),
        "log_norm": draw_log_norm(jax.random.fold_in(key_list[7], 71), 0),
        "positions": draw_positions(jax.random.fold_in(key_list[7], 71), 0),
    }


def reference(queries, key_rows, value_rows, output, out_grad, log_norm, positions):
    inv_root = 1.0 / math.sqrt(HD)
    rows_block = math.gcd(QTOK, 256)
    inner_blocks = QTOK // rows_block
    query_all = queries.astype(jnp.float32).reshape(N_PB, inner_blocks, rows_block, GROUP, HD)
    grad_all = out_grad.astype(jnp.float32).reshape(N_PB, inner_blocks, rows_block, GROUP, HD)
    saved_all = output.astype(jnp.float32).reshape(N_PB, inner_blocks, rows_block, GROUP, HD)
    key_all = key_rows.astype(jnp.float32)
    value_all = value_rows.astype(jnp.float32)
    row_delta = lax.optimization_barrier(jnp.sum(grad_all * saved_all, axis=4))
    norm_blocks = log_norm.T.reshape(N_PB, inner_blocks, rows_block, GROUP)
    pos_blocks = positions.reshape(N_PB, inner_blocks, rows_block)

    def one_block(running, inputs):
        key_sum, value_sum = running
        query_block, grad_block, delta_block, norm_block, pos_block = inputs
        scores = jnp.einsum('tgd,cd->tgc', query_block, key_all) * inv_root
        visible = (positions[None, :] <= pos_block[:, None])[:, None, :]
        probs_full = jnp.where(visible, jnp.exp(scores - norm_block[:, :, None]), jnp.float32(0.0))
        probs_low = lax.optimization_barrier(probs_full.astype(jnp.bfloat16)).astype(jnp.float32)
        value_sum = value_sum + jnp.einsum('tgc,tgd->cd', probs_low, grad_block)
        grad_probs = jnp.einsum('tgd,cd->tgc', grad_block, value_all)
        grad_scores = probs_full * (grad_probs - delta_block[:, :, None]) * inv_root
        grad_scores = lax.optimization_barrier(grad_scores.astype(jnp.bfloat16)).astype(jnp.float32)
        query_part = jnp.einsum('tgc,cd->tgd', grad_scores, key_all).reshape(rows_block, GROUP * HD)
        key_sum = key_sum + jnp.einsum('tgc,tgd->cd', grad_scores, query_block)
        return ((key_sum, value_sum), query_part)
    empty_grad = jnp.zeros((S, HD), jnp.float32)

    def one_stripe(totals, inputs):
        key_total, value_total = totals
        (key_sum, value_sum), query_parts = lax.scan(one_block, (empty_grad, empty_grad), inputs)
        return ((key_total + key_sum, value_total + value_sum), query_parts)
    (key_total, value_total), query_parts = lax.scan(one_stripe, (empty_grad, empty_grad), (query_all, grad_all, row_delta, norm_blocks, pos_blocks))
    return (query_parts.reshape(S, GROUP * HD), key_total, value_total)
```

```python
import functools
import math

import jax
import jax.numpy as jnp
from jax import lax
from jax.experimental import pallas as pl
from jax.experimental.pallas import tpu as pltpu
from jax.sharding import PartitionSpec as P

MESH = pl.DeviceIdType.MESH
LOG2E = math.log2(math.e)
HIDDEN = -1e30
GROUPED = 4
ALONG, UPWARD, STRAIGHT, RELAYED = range(4)
START, PASS, COMPUTE, ADD = range(4)
KEY_ROUTE = (
    (),
    (STRAIGHT, STRAIGHT, ALONG, ALONG),
    (STRAIGHT, STRAIGHT, ALONG, ALONG),
    (RELAYED, UPWARD, ALONG, UPWARD),
)
SUM_ROUTE = (
    (),
    (ALONG, STRAIGHT, ALONG, ALONG),
    (ALONG, STRAIGHT, ALONG, ALONG),
    (ALONG, UPWARD, ALONG, ALONG),
)
STEPS = (
    (START, 2, 0), (START, 0, 2), (START, 1, 1), (START, 1, 0), (PASS, 2, 0), (START, 0, 3), (START, 2, 1),
    (COMPUTE, (2, 0), (0, 0)), (PASS, 0, 2), (COMPUTE, (0, 2), (1, 0)), (PASS, 3, 0), (COMPUTE, (3, 0), (1, 1)),
    (START, 0, 1), (PASS, 0, 3), (COMPUTE, (2, 1), (1, 2)), (COMPUTE, (2, 2), (3, 2)), (COMPUTE, (3, 1), (3, 3)),
    (COMPUTE, (2, 3), (1, 3)), (ADD, 0, 2), (COMPUTE, (0, 1), (0, 3)), (ADD, 0, 1), (ADD, 0, 3), (ADD, 3, 0),
)


def flip(index, mask, count):
    total, bit = 0, 1
    while bit < count:
        digit = (index // bit) % 2
        total = total + bit * ((1 - digit) if mask & bit else digit)
        bit *= 2
    return total


def kernel(
    planes, layers, q_ref, k_ref, v_ref, o_ref, g_ref, n_ref, pos_ref,
    dq_ref, dkv_ref,
    q_all, g_all, o_own, kv_own, n_own, pos, kv_all, norm, delta, bias, dkv_acc, dq_acc, dq_in,
    own, out1, in1, out2, in2,
    load, pair_send, pair_recv, z_send, z_recv, p_send, p_recv, r1_send, r1_recv, r2_send, r2_recv,
):
    pb, z = lax.axis_index("pb"), lax.axis_index("kv")
    p, core = pb // 2, pb % 2
    rows, heads = q_ref.shape[0], n_ref.shape[0]
    keys, width = k_ref.shape
    part_rows = keys // 2
    inv_root = 1.0 / math.sqrt(width)

    loads = [
        pltpu.make_async_copy(src, dst, load.at[i])
        for i, (src, dst) in enumerate((
            (k_ref, kv_own.at[0]), (v_ref, kv_own.at[1]),
            (q_ref, q_all.at[pl.ds(0, rows)]), (g_ref, g_all.at[pl.ds(0, rows)]),
            (o_ref, o_own), (n_ref, n_own), (pos_ref, pos),
        ))
    ]
    for copy in loads:
        copy.start()

    partner = {"pb": p * 2 + 1 - core, "kv": z}
    z_peers = [(z + step) % layers for step in range(layers)]
    p_peers = [flip(p, step, planes) for step in range(planes)]

    def above(step):
        return {"pb": pb, "kv": z_peers[step]}

    def beside(step):
        return {"pb": p_peers[step] * 2 + core, "kv": z}

    def remote(src, dst, send, recv, device):
        return pltpu.make_async_remote_copy(
            src_ref=src, dst_ref=dst, send_sem=send, recv_sem=recv,
            device_id=device, device_id_type=MESH,
        )

    peers = [partner] + [above(s) for s in range(1, layers)] + [beside(s) for s in range(1, planes)]
    barrier = pltpu.get_barrier_semaphore()
    for peer in peers:
        pl.semaphore_signal(barrier, inc=1, device_id=peer, device_id_type=MESH)
    pl.semaphore_wait(barrier, len(peers))

    def place_of(layer):
        return pl.ds(pl.multiple_of(layer * part_rows, part_rows), part_rows)

    def own_part(half):
        return kv_own.at[:, pl.ds(half * part_rows, part_rows)]

    sent = []

    def start(copy):
        copy.start()
        sent.append(copy)
        return copy

    loads[0].wait()
    loads[1].wait()
    z_copies, p_copies = {}, {}
    for half in range(2):
        for step in range(1, layers):
            z_copies[half, step] = start(remote(
                own_part(half), kv_all.at[p, half, :, place_of(z)],
                z_send.at[half, step - 1], z_recv.at[half, step - 1], above(step),
            ))

    def spread(half, step_z, step):
        place = place_of((z + layers - step_z) % layers)
        landed = kv_all.at[p, half, :, place]
        p_copies[half, step_z, step] = start(remote(
            own_part(half) if step_z == 0 else landed, landed,
            p_send.at[half, step_z, step - 1], p_recv.at[half, step_z, step - 1], beside(step),
        ))

    relayed, waited = planes == 4, set()
    near = [step for step in range(1, planes) if step & (step - 1) == 0]
    far = [step for step in range(1, planes) if step & (step - 1)]
    for step in near:
        spread(0, 0, step)

    loads[2].wait()
    loads[3].wait()
    second = pl.ds(rows, rows)
    pair_copies = [
        start(remote(full.at[pl.ds(0, rows)], full.at[second], pair_send.at[i], pair_recv.at[i], partner))
        for i, full in enumerate((q_all, g_all))
    ]

    for copy in loads[4:]:
        copy.wait()
    norm[:, :rows] = n_own[...] * LOG2E
    for h in range(heads):
        part = slice(h * width, (h + 1) * width)
        product = g_all[:rows, part].astype(jnp.float32) * o_own[:, part].astype(jnp.float32)
        delta[h : h + 1, :rows] = jnp.sum(product.T, axis=0, keepdims=True)
    for i, stat in enumerate((norm, delta)):
        pair_copies.append(start(remote(
            stat.at[:, pl.ds(0, rows)], stat.at[:, second], pair_send.at[2 + i], pair_recv.at[2 + i], partner
        )))
    for half in range(2):
        kv_all[p, half, :, place_of(z)] = kv_own[:, half * part_rows : (half + 1) * part_rows]

    pos_own = pos[pl.ds(pb * layers + z, 1), :]
    pos_partner = pos[pl.ds((p * 2 + 1 - core) * layers + z, 1), :]

    def make_bias(column, carry):
        for layer in range(layers):
            row = pos[pl.ds(layer * (2 * planes) + column * 2 + core, 1), :]
            key_pos = jnp.broadcast_to(row, (rows, keys)).T
            place = slice(layer * part_rows, (layer + 1) * part_rows)
            for side, query_pos in enumerate((pos_own, pos_partner)):
                block = jnp.where(key_pos <= query_pos, 0.0, HIDDEN)
                for half in range(2):
                    bias[column, half, place, side * rows : (side + 1) * rows] = block[
                        half * part_rows : (half + 1) * part_rows
                    ]
        return carry

    def gather(half):
        for step_z in range(1, layers):
            z_copies[half, step_z].wait_recv()
            for step in near:
                spread(half, step_z, step)
        if relayed:
            return
        for step in far:
            for step_z in range(layers):
                spread(half, step_z, step)

    def relay(half):
        for i, source in enumerate(near):
            target = near[1 - i]
            for step_z in range(i * layers // 2, (i + 1) * layers // 2):
                p_copies[half, step_z, source].wait_recv()
                landed = kv_all.at[p_peers[source], half, :, place_of((z + layers - step_z) % layers)]
                p_copies[half, step_z, far[0]] = start(remote(
                    landed, landed,
                    p_send.at[half, step_z, far[0] - 1], p_recv.at[half, step_z, far[0] - 1], beside(target),
                ))
                waited.add((half, step_z, source))

    gather(0)
    for step in near:
        spread(1, 0, step)
    lax.fori_loop(0, planes, make_bias, 0)
    for copy in pair_copies:
        copy.wait_recv()

    last = (((1,), (1,)), ((), ()))

    def compute(column, half, first):
        keys_turned = kv_all[column, half, 0].T

        def one_head(h):
            part = pl.ds(pl.multiple_of(h * width, width), width)
            q, g = q_all[:, part], g_all[:, part]
            scores = lax.dot_general(kv_all[column, half, 0], q, last, preferred_element_type=jnp.float32)
            grad_probs = lax.dot_general(kv_all[column, half, 1], g, last, preferred_element_type=jnp.float32)
            probs = jnp.exp2(scores * (inv_root * LOG2E) - norm[pl.ds(h, 1), :] + bias[column, half])
            probs_low = probs.astype(jnp.bfloat16)
            grad_scores = (probs * (grad_probs - delta[pl.ds(h, 1), :]) * inv_root).astype(jnp.bfloat16)
            dv = jnp.dot(probs_low, g, preferred_element_type=jnp.float32)
            dk = jnp.dot(grad_scores, q, preferred_element_type=jnp.float32)
            dq = jnp.dot(keys_turned, grad_scores, preferred_element_type=jnp.float32)
            return dk, dv, dq

        dkv_acc[...] = jnp.zeros_like(dkv_acc)

        def body(i, carry):
            results = [one_head(GROUPED * i + j) for j in range(GROUPED)]
            for side in range(2):
                dkv_acc[side] += sum(result[side] for result in results)
            for j in range(GROUPED):
                dq = results[j][2]
                for side in range(2):
                    piece = dq[:, side * rows : (side + 1) * rows]
                    if first:
                        dq_acc[side, GROUPED * i + j] = piece
                    else:
                        dq_acc[side, GROUPED * i + j] += piece
            return carry

        lax.fori_loop(0, heads // GROUPED, body, 0)

    r1_copies, r2_copies = {}, {}

    def compute_peer(half, step):
        for step_z in range(layers):
            if (half, step_z, step) not in waited:
                p_copies[half, step_z, step].wait_recv()
        compute(p_peers[step], half, False)
        out1[half, step - 1] = dkv_acc[...].astype(jnp.bfloat16)
        r1_copies[half, step] = start(remote(
            out1.at[half, step - 1], in1.at[half, step - 1],
            r1_send.at[half, step - 1], r1_recv.at[half, step - 1], beside(step),
        ))

    def compute_own(half, first):
        compute(p, half, first)
        own[half] = dkv_acc[...]

    def plane_sum(half, layer):
        place = place_of(layer)
        total = own[half, :, place]
        for step in range(1, planes):
            total = total + in1[half, step - 1, :, place].astype(jnp.float32)
        return total

    def reduce_plane(half):
        for step in range(1, planes):
            r1_copies[half, step].wait_recv()
        for step in range(1, layers):
            out2[half, step - 1] = plane_sum(half, z_peers[step]).astype(jnp.bfloat16)
            r2_copies[half, step] = start(remote(
                out2.at[half, step - 1], in2.at[half, step - 1],
                r2_send.at[half, step - 1], r2_recv.at[half, step - 1], above(step),
            ))

    compute_own(0, True)
    gather(1)
    if relayed:
        relay(0)
    order = near + far
    for step in order:
        compute_peer(0, step)
        if relayed and step == near[-1]:
            relay(1)
    for step in order:
        compute_peer(1, step)
        if step == order[-2]:
            reduce_plane(0)
    compute_own(1, False)
    back = start(remote(dq_acc.at[1], dq_in, pair_send.at[4], pair_recv.at[4], partner))
    reduce_plane(1)

    back.wait_recv()
    for h in range(heads):
        part = slice(h * width, (h + 1) * width)
        dq_ref[:, part] = (dq_acc[0, h] + dq_in[h]).T

    for half in range(2):
        total = plane_sum(half, z)
        for step in range(1, layers):
            r2_copies[half, step].wait_recv()
            total = total + in2[half, step - 1].astype(jnp.float32)
        dkv_ref[:, half * part_rows : (half + 1) * part_rows] = total
    for copy in sent:
        copy.wait_send()


def square(
    planes, layers, q_ref, k_ref, v_ref, o_ref, g_ref, n_ref, pos_ref,
    dq_ref, dkv_ref,
    q_all, g_all, o_own, n_own, pos, kv_all, norm, delta, bias, dq_acc, dq_in,
    own, out, into,
    load, pair_send, pair_recv, k_send, k_recv, s_send, s_recv,
):
    pb, z = lax.axis_index("pb"), lax.axis_index("kv")
    p, core = pb // 2, pb % 2
    rows, heads = q_ref.shape[0], n_ref.shape[0]
    keys, width = k_ref.shape
    inv_root = 1.0 / math.sqrt(width)
    low, full = jnp.bfloat16, jnp.float32
    here = (0, 0)

    loads = [
        pltpu.make_async_copy(src, dst, load.at[i])
        for i, (src, dst) in enumerate((
            (k_ref, kv_all.at[0, 0, 0]), (v_ref, kv_all.at[0, 0, 1]),
            (q_ref, q_all.at[pl.ds(0, rows)]), (g_ref, g_all.at[pl.ds(0, rows)]),
            (o_ref, o_own), (n_ref, n_own), (pos_ref, pos),
        ))
    ]
    for copy in loads:
        copy.start()

    partner = {"pb": p * 2 + 1 - core, "kv": z}
    z_peers = [flip(z, j, layers) for j in range(layers)]
    p_peers = [flip(p, c, planes) for c in range(planes)]

    def at(c, j):
        return {"pb": p_peers[c] * 2 + core, "kv": z_peers[j]}

    sent = []

    def send(src, dst, send_sem, recv_sem, device):
        copy = pltpu.make_async_remote_copy(
            src_ref=src, dst_ref=dst, send_sem=send_sem, recv_sem=recv_sem,
            device_id=device, device_id_type=MESH,
        )
        copy.start()
        sent.append(copy)
        return copy

    def across(j):
        return 1 + j % 2

    def sum_goes(c, j):
        if c == 0:
            return (0, j)
        return {ALONG: (c, 0), UPWARD: (0, j), STRAIGHT: (c, j), RELAYED: (across(j), 0)}[SUM_ROUTE[c][j]]

    def joins(c, j):
        if c == 0:
            return [(i, j) for i in range(1, planes) if SUM_ROUTE[i][j] == ALONG]
        found = [(c, i) for i in range(1, layers) if j == 0 and SUM_ROUTE[c][i] == UPWARD]
        if c == 3 - across(j) and SUM_ROUTE[3][j] == RELAYED:
            found.append((3, j))
        return found

    def key_hops(c, j):
        hops = []
        if c == 0 and j:
            hops += [(i, 0) for i in range(1, planes) if KEY_ROUTE[i][j] == ALONG]
        if c and j == 0:
            hops += [(0, i) for i in range(1, layers) if KEY_ROUTE[c][i] == UPWARD]
        if c == 3 - across(j) and KEY_ROUTE[3][j] == RELAYED:
            hops.append((3 - c, 0))
        return hops

    units = [(c, j) for c in range(planes) for j in range(layers)]
    starts = [step[1:] for step in STEPS if step[0] == START]
    peers = {*starts, *(hop for unit in units for hop in key_hops(*unit)), *(sum_goes(*unit) for unit in units)}
    peers = [partner] + [at(*peer) for peer in sorted(peers - {here})]
    barrier = pltpu.get_barrier_semaphore()
    for peer in peers:
        pl.semaphore_signal(barrier, inc=1, device_id=peer, device_id_type=MESH)
    pl.semaphore_wait(barrier, len(peers))

    coming = {}

    def give(unit, hop):
        c, j = unit[0] ^ hop[0], unit[1] ^ hop[1]
        coming[c, j] = send(kv_all.at[unit], kv_all.at[c, j], k_send.at[c, j], k_recv.at[c, j], at(*hop))

    def arrive(unit):
        if unit in coming:
            coming.pop(unit).wait_recv()

    loads[0].wait()
    loads[1].wait()
    for unit in starts:
        give(here, unit)

    loads[2].wait()
    loads[3].wait()
    second = pl.ds(rows, rows)
    pair_copies = [
        send(ref.at[pl.ds(0, rows)], ref.at[second], pair_send.at[i], pair_recv.at[i], partner)
        for i, ref in enumerate((q_all, g_all))
    ]
    for copy in loads[4:]:
        copy.wait()
    norm[:, :rows] = n_own[...] * LOG2E
    for h in range(heads):
        part = slice(h * width, (h + 1) * width)
        product = g_all[:rows, part].astype(full) * o_own[:, part].astype(full)
        delta[h : h + 1, :rows] = jnp.sum(product.T, axis=0, keepdims=True)
    for i, stat in enumerate((norm, delta)):
        pair_copies.append(send(
            stat.at[:, pl.ds(0, rows)], stat.at[:, second], pair_send.at[2 + i], pair_recv.at[2 + i], partner
        ))

    pos_own = pos[pl.ds(pb * layers + z, 1), :]
    pos_partner = pos[pl.ds((p * 2 + 1 - core) * layers + z, 1), :]
    for c, j in units:
        row = pos[pl.ds(z_peers[j] * (2 * planes) + p_peers[c] * 2 + core, 1), :]
        key_pos = jnp.broadcast_to(row, (rows, keys)).T
        for side, query_pos in enumerate((pos_own, pos_partner)):
            bias[c, j, :, side * rows : (side + 1) * rows] = jnp.where(key_pos <= query_pos, 0.0, HIDDEN)
    for copy in pair_copies:
        copy.wait_recv()

    last = (((1,), (1,)), ((), ()))

    def compute(chunk, first):
        def both(pick):
            return jnp.concatenate([pick(c, j) for c, j in chunk], axis=0)

        k = both(lambda c, j: kv_all[c, j, 0])
        v = both(lambda c, j: kv_all[c, j, 1])
        hidden = both(lambda c, j: bias[c, j])
        turned = k.T
        sums = None
        for h in range(heads):
            part = slice(h * width, (h + 1) * width)
            q, g = q_all[:, part], g_all[:, part]
            scores = lax.dot_general(k, q, last, preferred_element_type=full)
            grad_probs = lax.dot_general(v, g, last, preferred_element_type=full)
            probs = jnp.exp2(scores * (inv_root * LOG2E) - norm[h : h + 1, :] + hidden)
            grad_scores = (probs * (grad_probs - delta[h : h + 1, :]) * inv_root).astype(low)
            dv = jnp.dot(probs.astype(low), g, preferred_element_type=full)
            dk = jnp.dot(grad_scores, q, preferred_element_type=full)
            dq = jnp.dot(turned, grad_scores, preferred_element_type=full)
            sums = (dk, dv) if sums is None else (sums[0] + dk, sums[1] + dv)
            for side in range(2):
                piece = dq[:, side * rows : (side + 1) * rows]
                if first:
                    dq_acc[side, h] = piece
                else:
                    dq_acc[side, h] += piece
        for i, (c, j) in enumerate(chunk):
            place = own if keeps(c, j) else out
            for side, total in enumerate(sums):
                place[c, j, side] = total[i * keys : (i + 1) * keys].astype(place.dtype)

    def keeps(c, j):
        return c == 0 or len(joins(c, j)) > 0

    summed = {}

    def total_of(unit, others):
        total = own[unit]
        for other in others:
            summed[other].wait_recv()
            total = total + into[other].astype(full)
        return total

    def ship(unit):
        summed[unit] = send(out.at[unit], into.at[unit], s_send.at[unit], s_recv.at[unit], at(*sum_goes(*unit)))

    first = True
    for step in STEPS:
        if step[0] == PASS:
            unit = step[1:]
            hops = key_hops(*unit)
            if hops:
                arrive(unit)
            for hop in hops:
                give(unit, hop)
        elif step[0] == COMPUTE:
            chunk = step[1:]
            for unit in chunk:
                arrive(unit)
            compute(chunk, first)
            first = False
            for unit in chunk:
                if not keeps(*unit):
                    ship(unit)
        elif step[0] == ADD:
            unit = step[1:]
            if keeps(*unit):
                out[unit] = total_of(unit, joins(*unit)).astype(low)
                ship(unit)

    back = send(dq_acc.at[1], dq_in, pair_send.at[4], pair_recv.at[4], partner)
    back.wait_recv()
    for h in range(heads):
        part = slice(h * width, (h + 1) * width)
        dq_ref[:, part] = (dq_acc[0, h] + dq_in[h]).T
    arrivals = [unit for unit in units if unit != here and (unit[0] == 0 or SUM_ROUTE[unit[0]][unit[1]] == STRAIGHT)]
    dkv_ref[...] = total_of(here, arrivals + joins(*here))
    for copy in sent:
        copy.wait_send()


def finish(dq_in, dkv_in, dq_ref, dk_ref, dv_ref):
    dq_ref[...] = dq_in[...]
    dk_ref[...] = dkv_in[0]
    dv_ref[...] = dkv_in[1]


def solution(mesh):
    planes, layers = mesh.shape["pb"] // 2, mesh.shape["kv"]
    paired = planes == 4 and layers == len(KEY_ROUTE[1])

    def step(queries, key_rows, value_rows, output, out_grad, log_norm, positions):
        rows, columns = queries.shape
        keys, width = key_rows.shape
        heads = log_norm.shape[0]
        part_rows = keys // 2
        column = layers * part_rows
        low, full = jnp.bfloat16, jnp.float32
        vmem, hbm = pl.BlockSpec(memory_space=pltpu.VMEM), pl.BlockSpec(memory_space=pl.ANY)
        dma = pltpu.SemaphoreType.DMA
        pos = positions.reshape(-1, rows)
        if paired:
            body = square
            scratch = [
                pltpu.VMEM((2 * rows, columns), low),
                pltpu.VMEM((2 * rows, columns), low),
                pltpu.VMEM((rows, columns), low),
                pltpu.VMEM(log_norm.shape, full),
                pltpu.VMEM(pos.shape, jnp.int32),
                pltpu.VMEM((planes, layers, 2, keys, width), low),
                pltpu.VMEM((heads, 2 * rows), full),
                pltpu.VMEM((heads, 2 * rows), full),
                pltpu.VMEM((planes, layers, keys, 2 * rows), full),
                pltpu.VMEM((2, heads, width, rows), full),
                pltpu.VMEM((heads, width, rows), full),
                pltpu.VMEM((planes, layers, 2, keys, width), full),
                pltpu.VMEM((planes, layers, 2, keys, width), low),
                pltpu.VMEM((planes, layers, 2, keys, width), low),
                dma((7,)), dma((5,)), dma((5,)),
                dma((planes, layers)), dma((planes, layers)),
                dma((planes, layers)), dma((planes, layers)),
            ]
        else:
            body = kernel
            scratch = [
                pltpu.VMEM((2 * rows, columns), low),
                pltpu.VMEM((2 * rows, columns), low),
                pltpu.VMEM((rows, columns), low),
                pltpu.VMEM((2, keys, width), low),
                pltpu.VMEM(log_norm.shape, full),
                pltpu.VMEM(pos.shape, jnp.int32),
                pltpu.VMEM((planes, 2, 2, column, width), low),
                pltpu.VMEM((heads, 2 * rows), full),
                pltpu.VMEM((heads, 2 * rows), full),
                pltpu.VMEM((planes, 2, column, 2 * rows), full),
                pltpu.VMEM((2, column, width), full),
                pltpu.VMEM((2, heads, width, rows), full),
                pltpu.VMEM((heads, width, rows), full),
                pltpu.VMEM((2, 2, column, width), full),
                pltpu.VMEM((2, planes - 1, 2, column, width), low),
                pltpu.VMEM((2, planes - 1, 2, column, width), low),
                pltpu.VMEM((2, layers - 1, 2, part_rows, width), low),
                pltpu.VMEM((2, layers - 1, 2, part_rows, width), low),
                dma((7,)), dma((5,)), dma((5,)),
                dma((2, layers - 1)), dma((2, layers - 1)),
                dma((2, layers, planes - 1)), dma((2, layers, planes - 1)),
                dma((2, planes - 1)), dma((2, planes - 1)),
                dma((2, layers - 1)), dma((2, layers - 1)),
            ]
        dq, dkv = pl.pallas_call(
            functools.partial(body, planes, layers),
            out_shape=(
                jax.ShapeDtypeStruct((rows, columns), full),
                jax.ShapeDtypeStruct((2, keys, width), full),
            ),
            in_specs=[hbm] * 7,
            out_specs=(vmem, vmem),
            scratch_shapes=scratch,
            compiler_params=pltpu.CompilerParams(
                collective_id=0, has_side_effects=True, vmem_limit_bytes=58 * 2**20
            ),
        )(queries, key_rows, value_rows, output, out_grad, log_norm, pos)
        return pl.pallas_call(
            finish,
            out_shape=(
                jax.ShapeDtypeStruct((rows, columns), full),
                jax.ShapeDtypeStruct((keys, width), full),
                jax.ShapeDtypeStruct((keys, width), full),
            ),
            in_specs=[vmem] * 2,
            out_specs=(vmem, vmem, vmem),
        )(dq, dkv)

    return jax.shard_map(
        step,
        mesh=mesh,
        in_specs=(
            P(("pb", "kv"), None),
            P(("kv", "pb"), None),
            P(("kv", "pb"), None),
            P(("pb", "kv"), None),
            P(("pb", "kv"), None),
            P(None, ("pb", "kv")),
            P(),
        ),
        out_specs=(P(("pb", "kv"), None), P(("kv", "pb"), None), P(("kv", "pb"), None)),
        check_vma=False,
    )
```

```python
import functools
import math

import jax
import jax.numpy as jnp
from jax import lax
from jax.experimental import pallas as pl
from jax.experimental.pallas import tpu as pltpu
from jax.sharding import PartitionSpec as P

MESH = pl.DeviceIdType.MESH
LOG2E = math.log2(math.e)
HIDDEN = -1e30
GROUPED = 4
ALONG, UPWARD, STRAIGHT, RELAYED = range(4)
START, PASS, COMPUTE, ADD = range(4)
KEY_ROUTE = (
    (),
    (STRAIGHT, STRAIGHT, ALONG, ALONG),
    (STRAIGHT, STRAIGHT, ALONG, ALONG),
    (STRAIGHT, UPWARD, ALONG, UPWARD),
)
SUM_ROUTE = (
    (),
    (ALONG, ALONG, ALONG, ALONG),
    (ALONG, ALONG, ALONG, ALONG),
    (ALONG, UPWARD, UPWARD, ALONG),
)
STEPS = (
    (START, 3, 0), (START, 2, 1), (START, 0, 2), (START, 2, 0), (START, 1, 1), (START, 0, 3), (PASS, 3, 0),
    (PASS, 0, 2), (COMPUTE, (2, 1), (0, 2), (3, 0), (0, 0)), (START, 1, 0), (PASS, 0, 3), (START, 0, 1),
    (COMPUTE, (1, 2), (2, 2), (1, 1)), (COMPUTE, (3, 2), (3, 3), (3, 1)), (COMPUTE, (2, 3), (1, 3)), (ADD, 0, 2),
    (COMPUTE, (0, 3), (0, 1), (1, 0), (2, 0)), (ADD, 3, 0), (ADD, 0, 3), (ADD, 0, 1),
)


def flip(index, mask, count):
    total, bit = 0, 1
    while bit < count:
        digit = (index // bit) % 2
        total = total + bit * ((1 - digit) if mask & bit else digit)
        bit *= 2
    return total


def kernel(
    planes, layers, q_ref, k_ref, v_ref, o_ref, g_ref, n_ref, pos_ref,
    dq_ref, dkv_ref,
    q_all, g_all, o_own, kv_own, n_own, pos, kv_all, norm, delta, bias, dkv_acc, dq_acc, dq_in,
    own, out1, in1, out2, in2,
    load, pair_send, pair_recv, z_send, z_recv, p_send, p_recv, r1_send, r1_recv, r2_send, r2_recv,
):
    pb, z = lax.axis_index("pb"), lax.axis_index("kv")
    p, core = pb // 2, pb % 2
    rows, heads = q_ref.shape[0], n_ref.shape[0]
    keys, width = k_ref.shape
    part_rows = keys // 2
    inv_root = 1.0 / math.sqrt(width)

    loads = [
        pltpu.make_async_copy(src, dst, load.at[i])
        for i, (src, dst) in enumerate((
            (k_ref, kv_own.at[0]), (v_ref, kv_own.at[1]),
            (q_ref, q_all.at[pl.ds(0, rows)]), (g_ref, g_all.at[pl.ds(0, rows)]),
            (o_ref, o_own), (n_ref, n_own), (pos_ref, pos),
        ))
    ]
    for copy in loads:
        copy.start()

    partner = {"pb": p * 2 + 1 - core, "kv": z}
    z_peers = [(z + step) % layers for step in range(layers)]
    p_peers = [flip(p, step, planes) for step in range(planes)]

    def above(step):
        return {"pb": pb, "kv": z_peers[step]}

    def beside(step):
        return {"pb": p_peers[step] * 2 + core, "kv": z}

    def remote(src, dst, send, recv, device):
        return pltpu.make_async_remote_copy(
            src_ref=src, dst_ref=dst, send_sem=send, recv_sem=recv,
            device_id=device, device_id_type=MESH,
        )

    peers = [partner] + [above(s) for s in range(1, layers)] + [beside(s) for s in range(1, planes)]
    barrier = pltpu.get_barrier_semaphore()
    for peer in peers:
        pl.semaphore_signal(barrier, inc=1, device_id=peer, device_id_type=MESH)
    pl.semaphore_wait(barrier, len(peers))

    def place_of(layer):
        return pl.ds(pl.multiple_of(layer * part_rows, part_rows), part_rows)

    def own_part(half):
        return kv_own.at[:, pl.ds(half * part_rows, part_rows)]

    sent = []

    def start(copy):
        copy.start()
        sent.append(copy)
        return copy

    loads[0].wait()
    loads[1].wait()
    z_copies, p_copies = {}, {}
    for half in range(2):
        for step in range(1, layers):
            z_copies[half, step] = start(remote(
                own_part(half), kv_all.at[p, half, :, place_of(z)],
                z_send.at[half, step - 1], z_recv.at[half, step - 1], above(step),
            ))

    def spread(half, step_z, step):
        place = place_of((z + layers - step_z) % layers)
        landed = kv_all.at[p, half, :, place]
        p_copies[half, step_z, step] = start(remote(
            own_part(half) if step_z == 0 else landed, landed,
            p_send.at[half, step_z, step - 1], p_recv.at[half, step_z, step - 1], beside(step),
        ))

    relayed, waited = planes == 4, set()
    near = [step for step in range(1, planes) if step & (step - 1) == 0]
    far = [step for step in range(1, planes) if step & (step - 1)]
    for step in near:
        spread(0, 0, step)

    loads[2].wait()
    loads[3].wait()
    second = pl.ds(rows, rows)
    pair_copies = [
        start(remote(full.at[pl.ds(0, rows)], full.at[second], pair_send.at[i], pair_recv.at[i], partner))
        for i, full in enumerate((q_all, g_all))
    ]

    for copy in loads[4:]:
        copy.wait()
    norm[:, :rows] = n_own[...] * LOG2E
    for h in range(heads):
        part = slice(h * width, (h + 1) * width)
        product = g_all[:rows, part].astype(jnp.float32) * o_own[:, part].astype(jnp.float32)
        delta[h : h + 1, :rows] = jnp.sum(product.T, axis=0, keepdims=True)
    for i, stat in enumerate((norm, delta)):
        pair_copies.append(start(remote(
            stat.at[:, pl.ds(0, rows)], stat.at[:, second], pair_send.at[2 + i], pair_recv.at[2 + i], partner
        )))
    for half in range(2):
        kv_all[p, half, :, place_of(z)] = kv_own[:, half * part_rows : (half + 1) * part_rows]

    pos_own = pos[pl.ds(pb * layers + z, 1), :]
    pos_partner = pos[pl.ds((p * 2 + 1 - core) * layers + z, 1), :]

    def make_bias(column, carry):
        for layer in range(layers):
            row = pos[pl.ds(layer * (2 * planes) + column * 2 + core, 1), :]
            key_pos = jnp.broadcast_to(row, (rows, keys)).T
            place = slice(layer * part_rows, (layer + 1) * part_rows)
            for side, query_pos in enumerate((pos_own, pos_partner)):
                block = jnp.where(key_pos <= query_pos, 0.0, HIDDEN)
                for half in range(2):
                    bias[column, half, place, side * rows : (side + 1) * rows] = block[
                        half * part_rows : (half + 1) * part_rows
                    ]
        return carry

    def gather(half):
        for step_z in range(1, layers):
            z_copies[half, step_z].wait_recv()
            for step in near:
                spread(half, step_z, step)
        if relayed:
            return
        for step in far:
            for step_z in range(layers):
                spread(half, step_z, step)

    def relay(half):
        for i, source in enumerate(near):
            target = near[1 - i]
            for step_z in range(i * layers // 2, (i + 1) * layers // 2):
                p_copies[half, step_z, source].wait_recv()
                landed = kv_all.at[p_peers[source], half, :, place_of((z + layers - step_z) % layers)]
                p_copies[half, step_z, far[0]] = start(remote(
                    landed, landed,
                    p_send.at[half, step_z, far[0] - 1], p_recv.at[half, step_z, far[0] - 1], beside(target),
                ))
                waited.add((half, step_z, source))

    gather(0)
    for step in near:
        spread(1, 0, step)
    lax.fori_loop(0, planes, make_bias, 0)
    for copy in pair_copies:
        copy.wait_recv()

    last = (((1,), (1,)), ((), ()))

    def compute(column, half, first):
        keys_turned = kv_all[column, half, 0].T

        def one_head(h):
            part = pl.ds(pl.multiple_of(h * width, width), width)
            q, g = q_all[:, part], g_all[:, part]
            scores = lax.dot_general(kv_all[column, half, 0], q, last, preferred_element_type=jnp.float32)
            grad_probs = lax.dot_general(kv_all[column, half, 1], g, last, preferred_element_type=jnp.float32)
            probs = jnp.exp2(scores * (inv_root * LOG2E) - norm[pl.ds(h, 1), :] + bias[column, half])
            probs_low = probs.astype(jnp.bfloat16)
            grad_scores = (probs * (grad_probs - delta[pl.ds(h, 1), :]) * inv_root).astype(jnp.bfloat16)
            dv = jnp.dot(probs_low, g, preferred_element_type=jnp.float32)
            dk = jnp.dot(grad_scores, q, preferred_element_type=jnp.float32)
            dq = jnp.dot(keys_turned, grad_scores, preferred_element_type=jnp.float32)
            return dk, dv, dq

        dkv_acc[...] = jnp.zeros_like(dkv_acc)

        def body(i, carry):
            results = [one_head(GROUPED * i + j) for j in range(GROUPED)]
            for side in range(2):
                dkv_acc[side] += sum(result[side] for result in results)
            for j in range(GROUPED):
                dq = results[j][2]
                for side in range(2):
                    piece = dq[:, side * rows : (side + 1) * rows]
                    if first:
                        dq_acc[side, GROUPED * i + j] = piece
                    else:
                        dq_acc[side, GROUPED * i + j] += piece
            return carry

        lax.fori_loop(0, heads // GROUPED, body, 0)

    r1_copies, r2_copies = {}, {}

    def compute_peer(half, step):
        for step_z in range(layers):
            if (half, step_z, step) not in waited:
                p_copies[half, step_z, step].wait_recv()
        compute(p_peers[step], half, False)
        out1[half, step - 1] = dkv_acc[...].astype(jnp.bfloat16)
        r1_copies[half, step] = start(remote(
            out1.at[half, step - 1], in1.at[half, step - 1],
            r1_send.at[half, step - 1], r1_recv.at[half, step - 1], beside(step),
        ))

    def compute_own(half, first):
        compute(p, half, first)
        own[half] = dkv_acc[...]

    def plane_sum(half, layer):
        place = place_of(layer)
        total = own[half, :, place]
        for step in range(1, planes):
            total = total + in1[half, step - 1, :, place].astype(jnp.float32)
        return total

    def reduce_plane(half):
        for step in range(1, planes):
            r1_copies[half, step].wait_recv()
        for step in range(1, layers):
            out2[half, step - 1] = plane_sum(half, z_peers[step]).astype(jnp.bfloat16)
            r2_copies[half, step] = start(remote(
                out2.at[half, step - 1], in2.at[half, step - 1],
                r2_send.at[half, step - 1], r2_recv.at[half, step - 1], above(step),
            ))

    compute_own(0, True)
    gather(1)
    if relayed:
        relay(0)
    order = near + far
    for step in order:
        compute_peer(0, step)
        if relayed and step == near[-1]:
            relay(1)
    for step in order:
        compute_peer(1, step)
        if step == order[-2]:
            reduce_plane(0)
    compute_own(1, False)
    back = start(remote(dq_acc.at[1], dq_in, pair_send.at[4], pair_recv.at[4], partner))
    reduce_plane(1)

    back.wait_recv()
    for h in range(heads):
        part = slice(h * width, (h + 1) * width)
        dq_ref[:, part] = (dq_acc[0, h] + dq_in[h]).T

    for half in range(2):
        total = plane_sum(half, z)
        for step in range(1, layers):
            r2_copies[half, step].wait_recv()
            total = total + in2[half, step - 1].astype(jnp.float32)
        dkv_ref[:, half * part_rows : (half + 1) * part_rows] = total
    for copy in sent:
        copy.wait_send()


def square(
    planes, layers, q_ref, k_ref, v_ref, o_ref, g_ref, n_ref, pos_ref,
    dq_ref, dkv_ref,
    q_all, g_all, o_own, n_own, pos, kv_all, norm, delta, bias, dq_acc, dq_in,
    own, out, into,
    load, pair_send, pair_recv, k_send, k_recv, s_send, s_recv,
):
    pb, z = lax.axis_index("pb"), lax.axis_index("kv")
    p, core = pb // 2, pb % 2
    rows, heads = q_ref.shape[0], n_ref.shape[0]
    keys, width = k_ref.shape
    inv_root = 1.0 / math.sqrt(width)
    low, full = jnp.bfloat16, jnp.float32
    here = (0, 0)

    loads = [
        pltpu.make_async_copy(src, dst, load.at[i])
        for i, (src, dst) in enumerate((
            (k_ref, kv_all.at[0, 0, 0]), (v_ref, kv_all.at[0, 0, 1]),
            (q_ref, q_all.at[pl.ds(0, rows)]), (g_ref, g_all.at[pl.ds(0, rows)]),
            (o_ref, o_own), (n_ref, n_own), (pos_ref, pos),
        ))
    ]
    for copy in loads:
        copy.start()

    partner = {"pb": p * 2 + 1 - core, "kv": z}
    z_peers = [flip(z, j, layers) for j in range(layers)]
    p_peers = [flip(p, c, planes) for c in range(planes)]

    def at(c, j):
        return {"pb": p_peers[c] * 2 + core, "kv": z_peers[j]}

    sent = []

    def send(src, dst, send_sem, recv_sem, device):
        copy = pltpu.make_async_remote_copy(
            src_ref=src, dst_ref=dst, send_sem=send_sem, recv_sem=recv_sem,
            device_id=device, device_id_type=MESH,
        )
        copy.start()
        sent.append(copy)
        return copy

    def across(j):
        return 1 + j % 2

    def sum_goes(c, j):
        if c == 0:
            return (0, j)
        return {ALONG: (c, 0), UPWARD: (0, j), STRAIGHT: (c, j), RELAYED: (across(j), 0)}[SUM_ROUTE[c][j]]

    def joins(c, j):
        if c == 0:
            return [(i, j) for i in range(1, planes) if SUM_ROUTE[i][j] == ALONG]
        found = [(c, i) for i in range(1, layers) if j == 0 and SUM_ROUTE[c][i] == UPWARD]
        if c == 3 - across(j) and SUM_ROUTE[3][j] == RELAYED:
            found.append((3, j))
        return found

    def key_hops(c, j):
        hops = []
        if c == 0 and j:
            hops += [(i, 0) for i in range(1, planes) if KEY_ROUTE[i][j] == ALONG]
        if c and j == 0:
            hops += [(0, i) for i in range(1, layers) if KEY_ROUTE[c][i] == UPWARD]
        if c == 3 - across(j) and KEY_ROUTE[3][j] == RELAYED:
            hops.append((3 - c, 0))
        return hops

    units = [(c, j) for c in range(planes) for j in range(layers)]
    starts = [step[1:] for step in STEPS if step[0] == START]
    early = [step[0] for step in STEPS].index(COMPUTE)
    peers = {*starts, *(hop for unit in units for hop in key_hops(*unit)), *(sum_goes(*unit) for unit in units)}
    peers = [partner] + [at(*peer) for peer in sorted(peers - {here})]
    barrier = pltpu.get_barrier_semaphore()
    for peer in peers:
        pl.semaphore_signal(barrier, inc=1, device_id=peer, device_id_type=MESH)
    pl.semaphore_wait(barrier, len(peers))

    coming = {}

    def give(unit, hop):
        c, j = unit[0] ^ hop[0], unit[1] ^ hop[1]
        coming[c, j] = send(kv_all.at[unit], kv_all.at[c, j], k_send.at[c, j], k_recv.at[c, j], at(*hop))

    def arrive(unit):
        if unit in coming:
            coming.pop(unit).wait_recv()

    loads[0].wait()
    loads[1].wait()
    for step in STEPS[:early]:
        if step[0] == START:
            give(here, step[1:])

    loads[2].wait()
    loads[3].wait()
    second = pl.ds(rows, rows)
    pair_copies = [
        send(ref.at[pl.ds(0, rows)], ref.at[second], pair_send.at[i], pair_recv.at[i], partner)
        for i, ref in enumerate((q_all, g_all))
    ]
    for copy in loads[4:]:
        copy.wait()
    norm[:, :rows] = n_own[...] * LOG2E
    for h in range(heads):
        part = slice(h * width, (h + 1) * width)
        product = g_all[:rows, part].astype(full) * o_own[:, part].astype(full)
        delta[h : h + 1, :rows] = jnp.sum(product.T, axis=0, keepdims=True)
    for i, stat in enumerate((norm, delta)):
        pair_copies.append(send(
            stat.at[:, pl.ds(0, rows)], stat.at[:, second], pair_send.at[2 + i], pair_recv.at[2 + i], partner
        ))

    pos_own = pos[pl.ds(pb * layers + z, 1), :]
    pos_partner = pos[pl.ds((p * 2 + 1 - core) * layers + z, 1), :]
    for c, j in units:
        row = pos[pl.ds(z_peers[j] * (2 * planes) + p_peers[c] * 2 + core, 1), :]
        key_pos = jnp.broadcast_to(row, (rows, keys)).T
        for side, query_pos in enumerate((pos_own, pos_partner)):
            bias[c, j, :, side * rows : (side + 1) * rows] = jnp.where(key_pos <= query_pos, 0.0, HIDDEN)
    for copy in pair_copies:
        copy.wait_recv()

    last = (((1,), (1,)), ((), ()))

    def compute(chunk, first):
        def both(pick):
            return jnp.concatenate([pick(c, j) for c, j in chunk], axis=0)

        k = both(lambda c, j: kv_all[c, j, 0])
        v = both(lambda c, j: kv_all[c, j, 1])
        hidden = both(lambda c, j: bias[c, j])
        turned = k.T
        sums = None
        for h in range(heads):
            part = slice(h * width, (h + 1) * width)
            q, g = q_all[:, part], g_all[:, part]
            scores = lax.dot_general(k, q, last, preferred_element_type=full)
            grad_probs = lax.dot_general(v, g, last, preferred_element_type=full)
            probs = jnp.exp2(scores * (inv_root * LOG2E) - norm[h : h + 1, :] + hidden)
            grad_scores = (probs * (grad_probs - delta[h : h + 1, :]) * inv_root).astype(low)
            dv = jnp.dot(probs.astype(low), g, preferred_element_type=full)
            dk = jnp.dot(grad_scores, q, preferred_element_type=full)
            dq = jnp.dot(turned, grad_scores, preferred_element_type=full)
            sums = (dk, dv) if sums is None else (sums[0] + dk, sums[1] + dv)
            for side in range(2):
                piece = dq[:, side * rows : (side + 1) * rows]
                if first:
                    dq_acc[side, h] = piece
                else:
                    dq_acc[side, h] += piece
        for i, (c, j) in enumerate(chunk):
            place = own if keeps(c, j) else out
            for side, total in enumerate(sums):
                place[c, j, side] = total[i * keys : (i + 1) * keys].astype(place.dtype)

    def keeps(c, j):
        return c == 0 or len(joins(c, j)) > 0

    summed = {}

    def total_of(unit, others):
        total = own[unit]
        for other in others:
            summed[other].wait_recv()
            total = total + into[other].astype(full)
        return total

    def ship(unit):
        summed[unit] = send(out.at[unit], into.at[unit], s_send.at[unit], s_recv.at[unit], at(*sum_goes(*unit)))

    first = True
    for place, step in enumerate(STEPS):
        if step[0] == START and place > early:
            give(here, step[1:])
        elif step[0] == PASS:
            unit = step[1:]
            hops = key_hops(*unit)
            if hops:
                arrive(unit)
            for hop in hops:
                give(unit, hop)
        elif step[0] == COMPUTE:
            chunk = step[1:]
            for unit in chunk:
                arrive(unit)
            compute(chunk, first)
            first = False
            for unit in chunk:
                if not keeps(*unit):
                    ship(unit)
        elif step[0] == ADD:
            unit = step[1:]
            if keeps(*unit):
                out[unit] = total_of(unit, joins(*unit)).astype(low)
                ship(unit)

    back = send(dq_acc.at[1], dq_in, pair_send.at[4], pair_recv.at[4], partner)
    back.wait_recv()
    for h in range(heads):
        part = slice(h * width, (h + 1) * width)
        dq_ref[:, part] = (dq_acc[0, h] + dq_in[h]).T
    arrivals = [unit for unit in units if unit != here and (unit[0] == 0 or SUM_ROUTE[unit[0]][unit[1]] == STRAIGHT)]
    dkv_ref[...] = total_of(here, arrivals + joins(*here))
    for copy in sent:
        copy.wait_send()


def finish(dq_in, dkv_in, dq_ref, dk_ref, dv_ref, sem):
    copies = [
        pltpu.make_async_copy(src, dst, sem.at[i])
        for i, (src, dst) in enumerate(((dq_in, dq_ref), (dkv_in.at[0], dk_ref), (dkv_in.at[1], dv_ref)))
    ]
    for copy in copies:
        copy.start()
    for copy in copies:
        copy.wait()


def solution(mesh):
    planes, layers = mesh.shape["pb"] // 2, mesh.shape["kv"]
    paired = planes == 4 and layers == len(KEY_ROUTE[1])

    def step(queries, key_rows, value_rows, output, out_grad, log_norm, positions):
        rows, columns = queries.shape
        keys, width = key_rows.shape
        heads = log_norm.shape[0]
        part_rows = keys // 2
        column = layers * part_rows
        low, full = jnp.bfloat16, jnp.float32
        vmem, hbm = pl.BlockSpec(memory_space=pltpu.VMEM), pl.BlockSpec(memory_space=pltpu.HBM)
        dma = pltpu.SemaphoreType.DMA
        pos = positions.reshape(-1, rows)
        if paired:
            body = square
            scratch = [
                pltpu.VMEM((2 * rows, columns), low),
                pltpu.VMEM((2 * rows, columns), low),
                pltpu.VMEM((rows, columns), low),
                pltpu.VMEM(log_norm.shape, full),
                pltpu.VMEM(pos.shape, jnp.int32),
                pltpu.VMEM((planes, layers, 2, keys, width), low),
                pltpu.VMEM((heads, 2 * rows), full),
                pltpu.VMEM((heads, 2 * rows), full),
                pltpu.VMEM((planes, layers, keys, 2 * rows), full),
                pltpu.VMEM((2, heads, width, rows), full),
                pltpu.VMEM((heads, width, rows), full),
                pltpu.VMEM((planes, layers, 2, keys, width), full),
                pltpu.VMEM((planes, layers, 2, keys, width), low),
                pltpu.VMEM((planes, layers, 2, keys, width), low),
                dma((7,)), dma((5,)), dma((5,)),
                dma((planes, layers)), dma((planes, layers)),
                dma((planes, layers)), dma((planes, layers)),
            ]
        else:
            body = kernel
            scratch = [
                pltpu.VMEM((2 * rows, columns), low),
                pltpu.VMEM((2 * rows, columns), low),
                pltpu.VMEM((rows, columns), low),
                pltpu.VMEM((2, keys, width), low),
                pltpu.VMEM(log_norm.shape, full),
                pltpu.VMEM(pos.shape, jnp.int32),
                pltpu.VMEM((planes, 2, 2, column, width), low),
                pltpu.VMEM((heads, 2 * rows), full),
                pltpu.VMEM((heads, 2 * rows), full),
                pltpu.VMEM((planes, 2, column, 2 * rows), full),
                pltpu.VMEM((2, column, width), full),
                pltpu.VMEM((2, heads, width, rows), full),
                pltpu.VMEM((heads, width, rows), full),
                pltpu.VMEM((2, 2, column, width), full),
                pltpu.VMEM((2, planes - 1, 2, column, width), low),
                pltpu.VMEM((2, planes - 1, 2, column, width), low),
                pltpu.VMEM((2, layers - 1, 2, part_rows, width), low),
                pltpu.VMEM((2, layers - 1, 2, part_rows, width), low),
                dma((7,)), dma((5,)), dma((5,)),
                dma((2, layers - 1)), dma((2, layers - 1)),
                dma((2, layers, planes - 1)), dma((2, layers, planes - 1)),
                dma((2, planes - 1)), dma((2, planes - 1)),
                dma((2, layers - 1)), dma((2, layers - 1)),
            ]
        dq, dkv = pl.pallas_call(
            functools.partial(body, planes, layers),
            out_shape=(
                jax.ShapeDtypeStruct((rows, columns), full),
                jax.ShapeDtypeStruct((2, keys, width), full),
            ),
            in_specs=[hbm] * 7,
            out_specs=(vmem, vmem),
            scratch_shapes=scratch,
            compiler_params=pltpu.CompilerParams(
                collective_id=0, has_side_effects=True, vmem_limit_bytes=(24 if paired else 58) * 2**20
            ),
        )(*(pltpu.with_memory_space_constraint(x, pltpu.HBM) for x in (
            queries, key_rows, value_rows, output, out_grad, log_norm, pos
        )))
        return pl.pallas_call(
            finish,
            out_shape=(
                jax.ShapeDtypeStruct((rows, columns), full),
                jax.ShapeDtypeStruct((keys, width), full),
                jax.ShapeDtypeStruct((keys, width), full),
            ),
            in_specs=[vmem] * 2,
            out_specs=(hbm, hbm, hbm),
            scratch_shapes=[dma((3,))],
            compiler_params=pltpu.CompilerParams(vmem_limit_bytes=4 * 2**20),
        )(dq, dkv)

    return jax.shard_map(
        step,
        mesh=mesh,
        in_specs=(
            P(("pb", "kv"), None),
            P(("kv", "pb"), None),
            P(("kv", "pb"), None),
            P(("pb", "kv"), None),
            P(("pb", "kv"), None),
            P(None, ("pb", "kv")),
            P(),
        ),
        out_specs=(P(("pb", "kv"), None), P(("kv", "pb"), None), P(("kv", "pb"), None)),
        check_vma=False,
    )
```

```python
import functools
import math

import jax
import jax.numpy as jnp
from jax import lax
from jax.experimental import pallas as pl
from jax.experimental.pallas import tpu as pltpu
from jax.sharding import PartitionSpec as P

MESH = pl.DeviceIdType.MESH
LOG2E = math.log2(math.e)
HIDDEN = -1e30
GROUPED = 4
ALONG, UPWARD, STRAIGHT, RELAYED = range(4)
START, PASS, COMPUTE, ADD = range(4)
KEY_ROUTE = (
    (),
    (STRAIGHT, STRAIGHT, ALONG, ALONG),
    (STRAIGHT, STRAIGHT, ALONG, ALONG),
    (STRAIGHT, UPWARD, UPWARD, ALONG),
)
SUM_ROUTE = (
    (),
    (ALONG, ALONG, ALONG, ALONG),
    (ALONG, ALONG, ALONG, ALONG),
    (ALONG, UPWARD, ALONG, UPWARD),
)
STEPS = (
    (START, 0, 3), (START, 2, 1), (START, 0, 2), (START, 3, 0), (START, 1, 1), (PASS, 3, 0), (PASS, 0, 3),
    (COMPUTE, (0, 3), (3, 0), (2, 1)), (START, 0, 1), (PASS, 0, 2), (START, 2, 0), (START, 1, 0),
    (COMPUTE, (1, 3), (2, 3), (1, 1)), (COMPUTE, (3, 3), (3, 2), (3, 1)), (COMPUTE, (2, 2), (0, 1), (1, 2)),
    (ADD, 0, 3), (ADD, 0, 1), (COMPUTE, (0, 0), (2, 0), (1, 0), (0, 2)), (ADD, 0, 2), (ADD, 3, 0),
)


def flip(index, mask, count):
    total, bit = 0, 1
    while bit < count:
        digit = (index // bit) % 2
        total = total + bit * ((1 - digit) if mask & bit else digit)
        bit *= 2
    return total


def kernel(
    planes, layers, q_ref, k_ref, v_ref, o_ref, g_ref, n_ref, pos_ref,
    dq_ref, dkv_ref,
    q_all, g_all, o_own, kv_own, n_own, pos, kv_all, norm, delta, bias, dkv_acc, dq_acc, dq_in,
    own, out1, in1, out2, in2,
    load, pair_send, pair_recv, z_send, z_recv, p_send, p_recv, r1_send, r1_recv, r2_send, r2_recv,
):
    pb, z = lax.axis_index("pb"), lax.axis_index("kv")
    p, core = pb // 2, pb % 2
    rows, heads = q_ref.shape[0], n_ref.shape[0]
    keys, width = k_ref.shape
    part_rows = keys // 2
    inv_root = 1.0 / math.sqrt(width)

    loads = [
        pltpu.make_async_copy(src, dst, load.at[i])
        for i, (src, dst) in enumerate((
            (k_ref, kv_own.at[0]), (v_ref, kv_own.at[1]),
            (q_ref, q_all.at[pl.ds(0, rows)]), (g_ref, g_all.at[pl.ds(0, rows)]),
            (o_ref, o_own), (n_ref, n_own), (pos_ref, pos),
        ))
    ]
    for copy in loads:
        copy.start()

    partner = {"pb": p * 2 + 1 - core, "kv": z}
    z_peers = [(z + step) % layers for step in range(layers)]
    p_peers = [flip(p, step, planes) for step in range(planes)]

    def above(step):
        return {"pb": pb, "kv": z_peers[step]}

    def beside(step):
        return {"pb": p_peers[step] * 2 + core, "kv": z}

    def remote(src, dst, send, recv, device):
        return pltpu.make_async_remote_copy(
            src_ref=src, dst_ref=dst, send_sem=send, recv_sem=recv,
            device_id=device, device_id_type=MESH,
        )

    peers = [partner] + [above(s) for s in range(1, layers)] + [beside(s) for s in range(1, planes)]
    barrier = pltpu.get_barrier_semaphore()
    for peer in peers:
        pl.semaphore_signal(barrier, inc=1, device_id=peer, device_id_type=MESH)
    pl.semaphore_wait(barrier, len(peers))

    def place_of(layer):
        return pl.ds(pl.multiple_of(layer * part_rows, part_rows), part_rows)

    def own_part(half):
        return kv_own.at[:, pl.ds(half * part_rows, part_rows)]

    sent = []

    def start(copy):
        copy.start()
        sent.append(copy)
        return copy

    loads[0].wait()
    loads[1].wait()
    z_copies, p_copies = {}, {}
    for half in range(2):
        for step in range(1, layers):
            z_copies[half, step] = start(remote(
                own_part(half), kv_all.at[p, half, :, place_of(z)],
                z_send.at[half, step - 1], z_recv.at[half, step - 1], above(step),
            ))

    def spread(half, step_z, step):
        place = place_of((z + layers - step_z) % layers)
        landed = kv_all.at[p, half, :, place]
        p_copies[half, step_z, step] = start(remote(
            own_part(half) if step_z == 0 else landed, landed,
            p_send.at[half, step_z, step - 1], p_recv.at[half, step_z, step - 1], beside(step),
        ))

    relayed, waited = planes == 4, set()
    near = [step for step in range(1, planes) if step & (step - 1) == 0]
    far = [step for step in range(1, planes) if step & (step - 1)]
    for step in near:
        spread(0, 0, step)

    loads[2].wait()
    loads[3].wait()
    second = pl.ds(rows, rows)
    pair_copies = [
        start(remote(full.at[pl.ds(0, rows)], full.at[second], pair_send.at[i], pair_recv.at[i], partner))
        for i, full in enumerate((q_all, g_all))
    ]

    for copy in loads[4:]:
        copy.wait()
    norm[:, :rows] = n_own[...] * LOG2E
    for h in range(heads):
        part = slice(h * width, (h + 1) * width)
        product = g_all[:rows, part].astype(jnp.float32) * o_own[:, part].astype(jnp.float32)
        delta[h : h + 1, :rows] = jnp.sum(product.T, axis=0, keepdims=True)
    for i, stat in enumerate((norm, delta)):
        pair_copies.append(start(remote(
            stat.at[:, pl.ds(0, rows)], stat.at[:, second], pair_send.at[2 + i], pair_recv.at[2 + i], partner
        )))
    for half in range(2):
        kv_all[p, half, :, place_of(z)] = kv_own[:, half * part_rows : (half + 1) * part_rows]

    pos_own = pos[pl.ds(pb * layers + z, 1), :]
    pos_partner = pos[pl.ds((p * 2 + 1 - core) * layers + z, 1), :]

    def make_bias(column, carry):
        for layer in range(layers):
            row = pos[pl.ds(layer * (2 * planes) + column * 2 + core, 1), :]
            key_pos = jnp.broadcast_to(row, (rows, keys)).T
            place = slice(layer * part_rows, (layer + 1) * part_rows)
            for side, query_pos in enumerate((pos_own, pos_partner)):
                block = jnp.where(key_pos <= query_pos, 0.0, HIDDEN)
                for half in range(2):
                    bias[column, half, place, side * rows : (side + 1) * rows] = block[
                        half * part_rows : (half + 1) * part_rows
                    ]
        return carry

    def gather(half):
        for step_z in range(1, layers):
            z_copies[half, step_z].wait_recv()
            for step in near:
                spread(half, step_z, step)
        if relayed:
            return
        for step in far:
            for step_z in range(layers):
                spread(half, step_z, step)

    def relay(half):
        for i, source in enumerate(near):
            target = near[1 - i]
            for step_z in range(i * layers // 2, (i + 1) * layers // 2):
                p_copies[half, step_z, source].wait_recv()
                landed = kv_all.at[p_peers[source], half, :, place_of((z + layers - step_z) % layers)]
                p_copies[half, step_z, far[0]] = start(remote(
                    landed, landed,
                    p_send.at[half, step_z, far[0] - 1], p_recv.at[half, step_z, far[0] - 1], beside(target),
                ))
                waited.add((half, step_z, source))

    gather(0)
    for step in near:
        spread(1, 0, step)
    lax.fori_loop(0, planes, make_bias, 0)
    for copy in pair_copies:
        copy.wait_recv()

    last = (((1,), (1,)), ((), ()))

    def compute(column, half, first):
        keys_turned = kv_all[column, half, 0].T

        def one_head(h):
            part = pl.ds(pl.multiple_of(h * width, width), width)
            q, g = q_all[:, part], g_all[:, part]
            scores = lax.dot_general(kv_all[column, half, 0], q, last, preferred_element_type=jnp.float32)
            grad_probs = lax.dot_general(kv_all[column, half, 1], g, last, preferred_element_type=jnp.float32)
            probs = jnp.exp2(scores * (inv_root * LOG2E) - norm[pl.ds(h, 1), :] + bias[column, half])
            probs_low = probs.astype(jnp.bfloat16)
            grad_scores = (probs * (grad_probs - delta[pl.ds(h, 1), :]) * inv_root).astype(jnp.bfloat16)
            dv = jnp.dot(probs_low, g, preferred_element_type=jnp.float32)
            dk = jnp.dot(grad_scores, q, preferred_element_type=jnp.float32)
            dq = jnp.dot(keys_turned, grad_scores, preferred_element_type=jnp.float32)
            return dk, dv, dq

        dkv_acc[...] = jnp.zeros_like(dkv_acc)

        def body(i, carry):
            results = [one_head(GROUPED * i + j) for j in range(GROUPED)]
            for side in range(2):
                dkv_acc[side] += sum(result[side] for result in results)
            for j in range(GROUPED):
                dq = results[j][2]
                for side in range(2):
                    piece = dq[:, side * rows : (side + 1) * rows]
                    if first:
                        dq_acc[side, GROUPED * i + j] = piece
                    else:
                        dq_acc[side, GROUPED * i + j] += piece
            return carry

        lax.fori_loop(0, heads // GROUPED, body, 0)

    r1_copies, r2_copies = {}, {}

    def compute_peer(half, step):
        for step_z in range(layers):
            if (half, step_z, step) not in waited:
                p_copies[half, step_z, step].wait_recv()
        compute(p_peers[step], half, False)
        out1[half, step - 1] = dkv_acc[...].astype(jnp.bfloat16)
        r1_copies[half, step] = start(remote(
            out1.at[half, step - 1], in1.at[half, step - 1],
            r1_send.at[half, step - 1], r1_recv.at[half, step - 1], beside(step),
        ))

    def compute_own(half, first):
        compute(p, half, first)
        own[half] = dkv_acc[...]

    def plane_sum(half, layer):
        place = place_of(layer)
        total = own[half, :, place]
        for step in range(1, planes):
            total = total + in1[half, step - 1, :, place].astype(jnp.float32)
        return total

    def reduce_plane(half):
        for step in range(1, planes):
            r1_copies[half, step].wait_recv()
        for step in range(1, layers):
            out2[half, step - 1] = plane_sum(half, z_peers[step]).astype(jnp.bfloat16)
            r2_copies[half, step] = start(remote(
                out2.at[half, step - 1], in2.at[half, step - 1],
                r2_send.at[half, step - 1], r2_recv.at[half, step - 1], above(step),
            ))

    compute_own(0, True)
    gather(1)
    if relayed:
        relay(0)
    order = near + far
    for step in order:
        compute_peer(0, step)
        if relayed and step == near[-1]:
            relay(1)
    for step in order:
        compute_peer(1, step)
        if step == order[-2]:
            reduce_plane(0)
    compute_own(1, False)
    back = start(remote(dq_acc.at[1], dq_in, pair_send.at[4], pair_recv.at[4], partner))
    reduce_plane(1)

    back.wait_recv()
    for h in range(heads):
        part = slice(h * width, (h + 1) * width)
        dq_ref[:, part] = (dq_acc[0, h] + dq_in[h]).T

    for half in range(2):
        total = plane_sum(half, z)
        for step in range(1, layers):
            r2_copies[half, step].wait_recv()
            total = total + in2[half, step - 1].astype(jnp.float32)
        dkv_ref[:, half * part_rows : (half + 1) * part_rows] = total
    for copy in sent:
        copy.wait_send()


def square(
    planes, layers, q_ref, k_ref, v_ref, o_ref, g_ref, n_ref, pos_ref,
    dq_ref, dkv_ref,
    q_all, g_all, o_own, n_own, pos, kv_all, norm, delta, bias, dq_acc, dq_in,
    own, out, into,
    load, pair_send, pair_recv, k_send, k_recv, s_send, s_recv,
):
    pb, z = lax.axis_index("pb"), lax.axis_index("kv")
    p, core = pb // 2, pb % 2
    rows, heads = q_ref.shape[0], n_ref.shape[0]
    keys, width = k_ref.shape
    inv_root = 1.0 / math.sqrt(width)
    low, full = jnp.bfloat16, jnp.float32
    here = (0, 0)

    loads = [
        pltpu.make_async_copy(src, dst, load.at[i])
        for i, (src, dst) in enumerate((
            (k_ref, kv_all.at[0, 0, 0]), (v_ref, kv_all.at[0, 0, 1]),
            (q_ref, q_all.at[pl.ds(0, rows)]), (g_ref, g_all.at[pl.ds(0, rows)]),
            (o_ref, o_own), (n_ref, n_own), (pos_ref, pos),
        ))
    ]
    for copy in loads:
        copy.start()

    partner = {"pb": p * 2 + 1 - core, "kv": z}
    z_peers = [flip(z, j, layers) for j in range(layers)]
    p_peers = [flip(p, c, planes) for c in range(planes)]

    def at(c, j):
        return {"pb": p_peers[c] * 2 + core, "kv": z_peers[j]}

    sent = []

    def send(src, dst, send_sem, recv_sem, device):
        copy = pltpu.make_async_remote_copy(
            src_ref=src, dst_ref=dst, send_sem=send_sem, recv_sem=recv_sem,
            device_id=device, device_id_type=MESH,
        )
        copy.start()
        sent.append(copy)
        return copy

    def across(j):
        return 1 + j % 2

    def sum_goes(c, j):
        if c == 0:
            return (0, j)
        return {ALONG: (c, 0), UPWARD: (0, j), STRAIGHT: (c, j), RELAYED: (across(j), 0)}[SUM_ROUTE[c][j]]

    def joins(c, j):
        if c == 0:
            return [(i, j) for i in range(1, planes) if SUM_ROUTE[i][j] == ALONG]
        found = [(c, i) for i in range(1, layers) if j == 0 and SUM_ROUTE[c][i] == UPWARD]
        if c == 3 - across(j) and SUM_ROUTE[3][j] == RELAYED:
            found.append((3, j))
        return found

    def key_hops(c, j):
        hops = []
        if c == 0 and j:
            hops += [(i, 0) for i in range(1, planes) if KEY_ROUTE[i][j] == ALONG]
        if c and j == 0:
            hops += [(0, i) for i in range(1, layers) if KEY_ROUTE[c][i] == UPWARD]
        if c == 3 - across(j) and KEY_ROUTE[3][j] == RELAYED:
            hops.append((3 - c, 0))
        return hops

    units = [(c, j) for c in range(planes) for j in range(layers)]
    starts = [step[1:] for step in STEPS if step[0] == START]
    early = [step[0] for step in STEPS].index(COMPUTE)
    peers = {*starts, *(hop for unit in units for hop in key_hops(*unit)), *(sum_goes(*unit) for unit in units)}
    peers = [partner] + [at(*peer) for peer in sorted(peers - {here})]
    barrier = pltpu.get_barrier_semaphore()
    for peer in peers:
        pl.semaphore_signal(barrier, inc=1, device_id=peer, device_id_type=MESH)
    pl.semaphore_wait(barrier, len(peers))

    coming = {}

    def give(unit, hop):
        c, j = unit[0] ^ hop[0], unit[1] ^ hop[1]
        coming[c, j] = send(kv_all.at[unit], kv_all.at[c, j], k_send.at[c, j], k_recv.at[c, j], at(*hop))

    def arrive(unit):
        if unit in coming:
            coming.pop(unit).wait_recv()

    loads[0].wait()
    loads[1].wait()
    for step in STEPS[:early]:
        if step[0] == START:
            give(here, step[1:])

    loads[2].wait()
    loads[3].wait()
    second = pl.ds(rows, rows)
    pair_copies = [
        send(ref.at[pl.ds(0, rows)], ref.at[second], pair_send.at[i], pair_recv.at[i], partner)
        for i, ref in enumerate((q_all, g_all))
    ]
    for copy in loads[4:]:
        copy.wait()
    norm[:, :rows] = n_own[...] * LOG2E
    for h in range(heads):
        part = slice(h * width, (h + 1) * width)
        product = g_all[:rows, part].astype(full) * o_own[:, part].astype(full)
        delta[h : h + 1, :rows] = jnp.sum(product.T, axis=0, keepdims=True)
    for i, stat in enumerate((norm, delta)):
        pair_copies.append(send(
            stat.at[:, pl.ds(0, rows)], stat.at[:, second], pair_send.at[2 + i], pair_recv.at[2 + i], partner
        ))

    pos_own = pos[pl.ds(pb * layers + z, 1), :]
    pos_partner = pos[pl.ds((p * 2 + 1 - core) * layers + z, 1), :]
    for c, j in units:
        row = pos[pl.ds(z_peers[j] * (2 * planes) + p_peers[c] * 2 + core, 1), :]
        key_pos = jnp.broadcast_to(row, (rows, keys)).T
        for side, query_pos in enumerate((pos_own, pos_partner)):
            bias[c, j, :, side * rows : (side + 1) * rows] = jnp.where(key_pos <= query_pos, 0.0, HIDDEN)
    for copy in pair_copies:
        copy.wait_recv()

    last = (((1,), (1,)), ((), ()))

    def compute(chunk, first):
        def both(pick):
            return jnp.concatenate([pick(c, j) for c, j in chunk], axis=0)

        k = both(lambda c, j: kv_all[c, j, 0])
        v = both(lambda c, j: kv_all[c, j, 1])
        hidden = both(lambda c, j: bias[c, j])
        turned = k.T
        sums = None
        for h in range(heads):
            part = slice(h * width, (h + 1) * width)
            q, g = q_all[:, part], g_all[:, part]
            scores = lax.dot_general(k, q, last, preferred_element_type=full)
            grad_probs = lax.dot_general(v, g, last, preferred_element_type=full)
            probs = jnp.exp2(scores * (inv_root * LOG2E) - norm[h : h + 1, :] + hidden)
            grad_scores = (probs * (grad_probs - delta[h : h + 1, :]) * inv_root).astype(low)
            dv = jnp.dot(probs.astype(low), g, preferred_element_type=full)
            dk = jnp.dot(grad_scores, q, preferred_element_type=full)
            dq = jnp.dot(turned, grad_scores, preferred_element_type=full)
            sums = (dk, dv) if sums is None else (sums[0] + dk, sums[1] + dv)
            for side in range(2):
                piece = dq[:, side * rows : (side + 1) * rows]
                if first:
                    dq_acc[side, h] = piece
                else:
                    dq_acc[side, h] += piece
        for i, (c, j) in enumerate(chunk):
            place = own if keeps(c, j) else out
            for side, total in enumerate(sums):
                place[c, j, side] = total[i * keys : (i + 1) * keys].astype(place.dtype)

    def keeps(c, j):
        return c == 0 or len(joins(c, j)) > 0

    summed = {}

    def total_of(unit, others):
        total = own[unit]
        for other in others:
            summed[other].wait_recv()
            total = total + into[other].astype(full)
        return total

    def ship(unit):
        summed[unit] = send(out.at[unit], into.at[unit], s_send.at[unit], s_recv.at[unit], at(*sum_goes(*unit)))

    first = True
    for place, step in enumerate(STEPS):
        if step[0] == START and place > early:
            give(here, step[1:])
        elif step[0] == PASS:
            unit = step[1:]
            hops = key_hops(*unit)
            if hops:
                arrive(unit)
            for hop in hops:
                give(unit, hop)
        elif step[0] == COMPUTE:
            chunk = step[1:]
            for unit in chunk:
                arrive(unit)
            compute(chunk, first)
            first = False
            for unit in chunk:
                if not keeps(*unit):
                    ship(unit)
        elif step[0] == ADD:
            unit = step[1:]
            if keeps(*unit):
                out[unit] = total_of(unit, joins(*unit)).astype(low)
                ship(unit)

    back = send(dq_acc.at[1], dq_in, pair_send.at[4], pair_recv.at[4], partner)
    back.wait_recv()
    for h in range(heads):
        part = slice(h * width, (h + 1) * width)
        dq_ref[:, part] = (dq_acc[0, h] + dq_in[h]).T
    arrivals = [unit for unit in units if unit != here and (unit[0] == 0 or SUM_ROUTE[unit[0]][unit[1]] == STRAIGHT)]
    dkv_ref[...] = total_of(here, arrivals + joins(*here))
    for copy in sent:
        copy.wait_send()


def finish(dq_in, dkv_in, dq_ref, dk_ref, dv_ref, sem):
    copies = [
        pltpu.make_async_copy(src, dst, sem.at[i])
        for i, (src, dst) in enumerate(((dq_in, dq_ref), (dkv_in.at[0], dk_ref), (dkv_in.at[1], dv_ref)))
    ]
    for copy in copies:
        copy.start()
    for copy in copies:
        copy.wait()


def solution(mesh):
    planes, layers = mesh.shape["pb"] // 2, mesh.shape["kv"]
    paired = planes == 4 and layers == len(KEY_ROUTE[1])

    def step(queries, key_rows, value_rows, output, out_grad, log_norm, positions):
        rows, columns = queries.shape
        keys, width = key_rows.shape
        heads = log_norm.shape[0]
        part_rows = keys // 2
        column = layers * part_rows
        low, full = jnp.bfloat16, jnp.float32
        vmem, hbm = pl.BlockSpec(memory_space=pltpu.VMEM), pl.BlockSpec(memory_space=pltpu.HBM)
        dma = pltpu.SemaphoreType.DMA
        pos = positions.reshape(-1, rows)
        if paired:
            body = square
            scratch = [
                pltpu.VMEM((2 * rows, columns), low),
                pltpu.VMEM((2 * rows, columns), low),
                pltpu.VMEM((rows, columns), low),
                pltpu.VMEM(log_norm.shape, full),
                pltpu.VMEM(pos.shape, jnp.int32),
                pltpu.VMEM((planes, layers, 2, keys, width), low),
                pltpu.VMEM((heads, 2 * rows), full),
                pltpu.VMEM((heads, 2 * rows), full),
                pltpu.VMEM((planes, layers, keys, 2 * rows), full),
                pltpu.VMEM((2, heads, width, rows), full),
                pltpu.VMEM((heads, width, rows), full),
                pltpu.VMEM((planes, layers, 2, keys, width), full),
                pltpu.VMEM((planes, layers, 2, keys, width), low),
                pltpu.VMEM((planes, layers, 2, keys, width), low),
                dma((7,)), dma((5,)), dma((5,)),
                dma((planes, layers)), dma((planes, layers)),
                dma((planes, layers)), dma((planes, layers)),
            ]
        else:
            body = kernel
            scratch = [
                pltpu.VMEM((2 * rows, columns), low),
                pltpu.VMEM((2 * rows, columns), low),
                pltpu.VMEM((rows, columns), low),
                pltpu.VMEM((2, keys, width), low),
                pltpu.VMEM(log_norm.shape, full),
                pltpu.VMEM(pos.shape, jnp.int32),
                pltpu.VMEM((planes, 2, 2, column, width), low),
                pltpu.VMEM((heads, 2 * rows), full),
                pltpu.VMEM((heads, 2 * rows), full),
                pltpu.VMEM((planes, 2, column, 2 * rows), full),
                pltpu.VMEM((2, column, width), full),
                pltpu.VMEM((2, heads, width, rows), full),
                pltpu.VMEM((heads, width, rows), full),
                pltpu.VMEM((2, 2, column, width), full),
                pltpu.VMEM((2, planes - 1, 2, column, width), low),
                pltpu.VMEM((2, planes - 1, 2, column, width), low),
                pltpu.VMEM((2, layers - 1, 2, part_rows, width), low),
                pltpu.VMEM((2, layers - 1, 2, part_rows, width), low),
                dma((7,)), dma((5,)), dma((5,)),
                dma((2, layers - 1)), dma((2, layers - 1)),
                dma((2, layers, planes - 1)), dma((2, layers, planes - 1)),
                dma((2, planes - 1)), dma((2, planes - 1)),
                dma((2, layers - 1)), dma((2, layers - 1)),
            ]
        dq, dkv = pl.pallas_call(
            functools.partial(body, planes, layers),
            out_shape=(
                jax.ShapeDtypeStruct((rows, columns), full),
                jax.ShapeDtypeStruct((2, keys, width), full),
            ),
            in_specs=[hbm] * 7,
            out_specs=(vmem, vmem),
            scratch_shapes=scratch,
            compiler_params=pltpu.CompilerParams(
                collective_id=0, has_side_effects=True, vmem_limit_bytes=(24 if paired else 58) * 2**20
            ),
        )(*(pltpu.with_memory_space_constraint(x, pltpu.HBM) for x in (
            queries, key_rows, value_rows, output, out_grad, log_norm, pos
        )))
        return pl.pallas_call(
            finish,
            out_shape=(
                jax.ShapeDtypeStruct((rows, columns), full),
                jax.ShapeDtypeStruct((keys, width), full),
                jax.ShapeDtypeStruct((keys, width), full),
            ),
            in_specs=[vmem] * 2,
            out_specs=(hbm, hbm, hbm),
            scratch_shapes=[dma((3,))],
            compiler_params=pltpu.CompilerParams(vmem_limit_bytes=4 * 2**20),
        )(dq, dkv)

    return jax.shard_map(
        step,
        mesh=mesh,
        in_specs=(
            P(("pb", "kv"), None),
            P(("kv", "pb"), None),
            P(("kv", "pb"), None),
            P(("pb", "kv"), None),
            P(("pb", "kv"), None),
            P(None, ("pb", "kv")),
            P(),
        ),
        out_specs=(P(("pb", "kv"), None), P(("kv", "pb"), None), P(("kv", "pb"), None)),
        check_vma=False,
    )
```
